512 devices in a mesh: seq: 128 (over y, x, z_lo, core), batch: 4 (over z_hi).
Axes of the slice: x: 4, y: 4, z: 16 (z_hi: 4, z_lo: 4; z = z_hi * 4 + z_lo), core: 2. Of those that a mesh axis runs over, the one named last changes fastest.
Arguments:
- values: bfloat16 [1, 32768, 512], P(None, 'seq', 'batch'), may hold values from -6 to 6
- gate_in: bfloat16 [1, 32768, 512], P(None, 'seq', 'batch'), may hold values from -6 to 6
- gate_out: bfloat16 [1, 32768, 512], P(None, 'seq', 'batch'), may hold values from -6 to 6
- cotangent: bfloat16 [1, 32768, 512], P(None, 'seq', 'batch'), may hold values from -6 to 6
- filters: float32 [64, 32768], P(None, 'seq'), may hold values from -0.03125 to 0.03125
Outputs:
- grad_values: bfloat16 [1, 32768, 512], P(None, 'seq', 'batch')
- grad_gate_in: bfloat16 [1, 32768, 512], P(None, 'seq', 'batch')
- grad_gate_out: bfloat16 [1, 32768, 512], P(None, 'seq', 'batch')
- grad_filters: float32 [64, 32768], P('batch', 'seq')
The draws below stay inside these ranges and needn't reach their ends.
All inputs are finite; a program needn't handle non-finite values.
Results may differ from the reference program's by a relative error of at most 0.012.
Values may be sent and summed in bfloat16 or wider, within the bound.
No kernel may reach another device: no remote copies, remote signals or barrier semaphores. Data moves between devices by JAX's collectives and lax.ppermute only.
A program may use at most 64 MiB of HBM per device.

```python
import jax
import jax.numpy as jnp
from jax import lax

CHANNELS = 512
FILTERS = 64
SEQS = 1
SEQ_LEN = 32768


def steps_of(key, dims, split, least, high):
    factor_of, own = 1.0, jax.random.fold_in(key, 6)
    for axis_at, parts in split:
        heights = jnp.exp(jax.random.uniform(jax.random.fold_in(own, axis_at), (parts,), jnp.float32, least / len(split), high / len(split)))
        factor_of = factor_of * jnp.repeat(heights, dims[axis_at] // parts).reshape([-1 if axis == axis_at else 1 for axis in range(len(dims))])
    return factor_of


def noise(key, extent, width, most, shards=(), kind=jnp.bfloat16):
    drawn = width * jax.random.normal(key, extent, jnp.float32)
    if shards:
        drawn = drawn * steps_of(key, extent, shards, -0.22, 0.18)
    return jnp.clip(drawn, -most, most).astype(kind)


def setup_inputs(seed: int = 0) -> dict:
    keys = jax.random.split(jax.random.key(seed), 6)
    values = noise(keys[0], (SEQS, SEQ_LEN, CHANNELS), 1.0, 6.0, ((1, 128), (2, 4)))
    gate_in = noise(keys[1], (SEQS, SEQ_LEN, CHANNELS), 1.0, 6.0, ((1, 128), (2, 4)))
    gate_out = noise(keys[2], (SEQS, SEQ_LEN, CHANNELS), 1.0, 6.0, ((1, 128), (2, 4)))
    cotangent = noise(keys[3], (SEQS, SEQ_LEN, CHANNELS), 1.0, 6.0, ((1, 128), (2, 4)))
    filters = noise(keys[4], (FILTERS, SEQ_LEN), SEQ_LEN ** -0.5, 0.03125, ((1, 128),), jnp.float32)
    return {"values": values, "gate_in": gate_in, "gate_out": gate_out, "cotangent": cotangent, "filters": filters}


def reference(values, gate_in, gate_out, cotangent, filters):
    shared = CHANNELS // FILTERS
    padded_len = 2 * SEQ_LEN
    mixed_in = (values.astype(jnp.float32) * gate_in.astype(jnp.float32)).astype(jnp.bfloat16)
    grad_mixed = (cotangent.astype(jnp.float32) * gate_out.astype(jnp.float32)).astype(jnp.bfloat16)

    def blocks(series):
        return jnp.transpose(series.astype(jnp.float32).reshape(SEQS, SEQ_LEN, shared, FILTERS), (2, 0, 3, 1))
    spec_tap = jnp.fft.rfft(filters, n=padded_len, axis=-1)

    def block_step(tap_total, pair):
        mixed_block, grad_block = pair
        spec_in = jnp.fft.rfft(mixed_block, n=padded_len, axis=-1)
        spec_grad = jnp.fft.rfft(grad_block, n=padded_len, axis=-1)
        conv_part = jnp.fft.irfft(spec_tap * spec_in, n=padded_len, axis=-1)[..., :SEQ_LEN].astype(jnp.bfloat16)
        back_part = jnp.fft.irfft(jnp.conj(spec_tap) * spec_grad, n=padded_len, axis=-1)[..., :SEQ_LEN].astype(jnp.bfloat16)
        tap_part = jnp.fft.irfft(jnp.conj(spec_in) * spec_grad, n=padded_len, axis=-1)[..., :SEQ_LEN]
        return (tap_total + lax.optimization_barrier(jnp.sum(tap_part, axis=0)), (conv_part, back_part))
    start_total = jnp.zeros((FILTERS, SEQ_LEN), jnp.float32)
    tap_total, (conv_blocks, back_blocks) = lax.scan(block_step, start_total, (blocks(mixed_in), blocks(grad_mixed)))
    conv_seq = jnp.transpose(conv_blocks, (1, 3, 0, 2)).reshape(SEQS, SEQ_LEN, CHANNELS).astype(jnp.float32)
    back_seq = jnp.transpose(back_blocks, (1, 3, 0, 2)).reshape(SEQS, SEQ_LEN, CHANNELS).astype(jnp.float32)
    grad_values = (gate_in.astype(jnp.float32) * back_seq).astype(jnp.bfloat16)
    grad_gate_in = (values.astype(jnp.float32) * back_seq).astype(jnp.bfloat16)
    grad_gate_out = (cotangent.astype(jnp.float32) * conv_seq).astype(jnp.bfloat16)
    factor = 1.0 / jnp.sqrt(jnp.float32(shared * SEQS * SEQ_LEN))
    grad_filters = (tap_total * factor).astype(jnp.float32)
    return (grad_values, grad_gate_in, grad_gate_out, grad_filters)
```

```python
import math

import jax
import jax.numpy as jnp
import ml_dtypes
import numpy as np
from jax import lax
from jax.experimental import pallas as pl
from jax.experimental.pallas import tpu as pltpu
from jax.sharding import PartitionSpec as P

F32 = jnp.float32
BF16 = jnp.bfloat16


def tables(rows, cols):
    n = rows * cols
    theta = 2.0 * np.pi * np.outer(np.arange(rows) + 0.25, np.arange(rows)) / rows
    first = np.concatenate([np.cos(theta), -np.sin(theta)], 0)
    phi = 2.0 * np.pi * np.outer(np.arange(rows) + 0.25, np.arange(cols)) / n
    turn = np.concatenate([np.cos(phi), np.sin(phi)], 1)
    angle = 2.0 * np.pi * (np.outer(np.arange(cols), np.arange(cols)) % cols) / cols
    c, s = np.cos(angle), np.sin(angle)
    inner = np.block([[c, -s], [s, c]])

    def short(a):
        return a.astype(np.float32).astype(ml_dtypes.bfloat16)

    return (
        short(first),
        short(np.ascontiguousarray(first.T)),
        turn.astype(np.float32),
        short(inner),
        short(np.ascontiguousarray(inner.T)),
    )


def dot(a, b):
    return jnp.dot(a, b, preferred_element_type=F32)


def vmem_call(kernel, out_shape, flops, size):
    return pl.pallas_call(
        kernel,
        out_shape=out_shape,
        cost_estimate=pl.CostEstimate(flops=flops, bytes_accessed=size, transcendentals=0),
    )


def gather_kernel(values, gate_in, gate_out, cotangent, filters, out):
    half = out.shape[1] // 6
    taps = filters.shape[0]
    for part, (a, b) in enumerate(((values, gate_in), (cotangent, gate_out))):
        product = a[...].astype(F32) * b[...].astype(F32)
        for side in range(2):
            piece = product[side * half : (side + 1) * half].T
            at = (3 * side + part) * half
            out[:, at : at + half] = piece.astype(BF16)
    for side in range(2):
        piece = filters[:, side * half : (side + 1) * half].astype(BF16)
        at = (3 * side + 2) * half
        for copy in range(out.shape[0] // taps):
            out[copy * taps : (copy + 1) * taps, at : at + half] = piece


def spectra_kernel(scale, sent, first, first_t, turn, inner, inner_t, out):
    rows = out.shape[0]
    cols = out.shape[1] // 3
    half = cols // 2
    wc, ws = turn[:, :cols], turn[:, cols:]
    a = dot(first[...], sent[...])
    specs = []
    for j in range(3):
        at = [slice(j * half, (j + 1) * half), slice((3 + j) * half, (4 + j) * half)]
        re = jnp.concatenate([a[:rows, at[0]], a[:rows, at[1]]], axis=1)
        im = jnp.concatenate([a[rows:, at[0]], a[rows:, at[1]]], axis=1)
        b = jnp.concatenate([re * wc + im * ws, im * wc - re * ws], axis=1)
        f = dot(b.astype(BF16), inner[...])
        specs.append((f[:, :cols], f[:, cols:]))
    (xr, xi), (gr, gi), (hr, hi) = specs
    products = (
        (hr * xr - hi * xi, hr * xi + hi * xr, 1.0),
        (hr * gr + hi * gi, hr * gi - hi * gr, 1.0),
        (xr * gr + xi * gi, xr * gi - xi * gr, scale),
    )
    size = 1.0 / (rows * cols)
    for j, (pr, pi, factor) in enumerate(products):
        p = jnp.concatenate([pr, pi], axis=1).astype(BF16)
        u = dot(p, inner_t[...])
        ur, ui = u[:, :cols], u[:, cols:]
        v = jnp.concatenate([ur * wc - ui * ws, ur * ws + ui * wc], axis=0)
        y = dot(first_t[...], v.astype(BF16)) * (size * factor)
        for side in range(2):
            at = (3 * side + j) * half
            out[:, at : at + half] = y[:, side * half : (side + 1) * half].astype(BF16)


def finish_kernel(values, gate_in, cotangent, back, grad_values, grad_gate_in, grad_gate_out):
    half = back.shape[1] // 6
    for side in range(2):
        at = slice(side * half, (side + 1) * half)
        lo = 3 * side * half
        conv = back[:, lo : lo + half].astype(F32).T
        corr = back[:, lo + half : lo + 2 * half].astype(F32).T
        grad_values[at] = (gate_in[at].astype(F32) * corr).astype(BF16)
        grad_gate_in[at] = (values[at].astype(F32) * corr).astype(BF16)
        grad_gate_out[at] = (cotangent[at].astype(F32) * conv).astype(BF16)


def body(values, gate_in, gate_out, cotangent, filters):
    values, gate_in, gate_out, cotangent = (x[0] for x in (values, gate_in, gate_out, cotangent))
    cols, channels = values.shape
    shards = lax.axis_size("seq")
    replicas = lax.axis_size("batch")
    taps = filters.shape[0]
    wide = 3 * cols
    first, first_t, turn, inner, inner_t = tables(shards, cols)
    scale = 1.0 / math.sqrt(channels * replicas // taps * shards * cols)

    def to_all(x):
        x = x.reshape(x.shape[0], 2, wide // 2)
        x = lax.all_to_all(x, "seq", split_axis=0, concat_axis=0, tiled=True)
        return x.reshape(x.shape[0], wide)

    pack = vmem_call(
        gather_kernel,
        jax.ShapeDtypeStruct((channels, wide), BF16),
        10 * channels * wide,
        12 * channels * wide,
    )
    sent = to_all(pack(values, gate_in, gate_out, cotangent, filters))

    def spectra(*refs):
        spectra_kernel(scale, *refs)

    transform = vmem_call(
        spectra,
        jax.ShapeDtypeStruct((shards, wide), BF16),
        4 * shards * wide * (2 * cols + shards),
        4 * shards * wide,
    )
    back = to_all(transform(sent, first, first_t, turn, inner, inner_t))

    half = cols // 2
    terms = jnp.concatenate([back[:, wide // 2 - half : wide // 2], back[:, wide - half :]], axis=1)
    per_filter = terms.astype(F32).reshape(channels // taps, taps, cols).sum(axis=0)
    parts = per_filter.astype(BF16).reshape(replicas, taps // replicas, cols)
    parts = lax.all_to_all(parts, "batch", split_axis=0, concat_axis=0, tiled=True)
    finish = vmem_call(
        finish_kernel,
        [jax.ShapeDtypeStruct((cols, channels), BF16)] * 3,
        12 * cols * channels,
        20 * cols * channels,
    )
    grads = finish(values, gate_in, cotangent, back)
    grad_filters = parts.astype(F32).sum(axis=0)
    return tuple(x[None] for x in grads) + (grad_filters,)


def solution(mesh):
    placed = P(None, "seq", "batch")
    return jax.shard_map(
        body,
        mesh=mesh,
        in_specs=(placed, placed, placed, placed, P(None, "seq")),
        out_specs=(placed, placed, placed, P("batch", "seq")),
        check_vma=False,
    )
```

```python
import math

import jax
import jax.numpy as jnp
import ml_dtypes
import numpy as np
from jax import lax
from jax.experimental import pallas as pl
from jax.experimental.pallas import tpu as pltpu
from jax.sharding import PartitionSpec as P

F32 = jnp.float32
BF16 = jnp.bfloat16
VMEM_LIMIT = 12 << 20
SEQ_FIRST = 2 * 32 + 2 * 8 + 1 * 2
BATCH_FIRST = 2


def tables(rows, cols, order):
    n = rows * cols
    theta = 2.0 * np.pi * np.outer(np.arange(rows) + 0.25, np.arange(rows)) / rows
    first = np.concatenate([np.cos(theta), -np.sin(theta)], 0)[:, order]
    phi = 2.0 * np.pi * np.outer(np.arange(rows) + 0.25, np.arange(cols)) / n
    turn = np.concatenate([np.cos(phi), np.sin(phi)], 1)
    angle = 2.0 * np.pi * (np.outer(np.arange(cols), np.arange(cols)) % cols) / cols
    c, s = np.cos(angle), np.sin(angle)
    inner = np.block([[c, -s], [s, c]])

    def short(a):
        return a.astype(np.float32).astype(ml_dtypes.bfloat16)

    return (
        short(first),
        short(np.ascontiguousarray(first.T)),
        turn.astype(np.float32),
        short(inner),
        short(np.ascontiguousarray(inner.T)),
    )


def dot(a, b):
    return jnp.dot(a, b, preferred_element_type=F32)


def vmem_call(kernel, out_shape, flops, size, **kwargs):
    return pl.pallas_call(
        kernel,
        out_shape=out_shape,
        compiler_params=pltpu.CompilerParams(vmem_limit_bytes=VMEM_LIMIT),
        cost_estimate=pl.CostEstimate(flops=flops, bytes_accessed=size, transcendentals=0),
        **kwargs,
    )


def gather_kernel(*refs):
    sources, out, held, sems = refs[:5], refs[5], refs[6:11], refs[11]
    copies = [pltpu.make_async_copy(s, h, sems.at[i]) for i, (s, h) in enumerate(zip(sources, held))]
    for copy in copies:
        copy.start()
    filters = held[4]
    half = out.shape[1] // 6
    taps = filters.shape[0]
    for part in range(2):
        a, b = held[2 * part : 2 * part + 2]
        copies[2 * part].wait()
        copies[2 * part + 1].wait()
        product = a[...].astype(F32) * b[...].astype(F32)
        for side in range(2):
            piece = product[side * half : (side + 1) * half].T
            at = (3 * side + part) * half
            out[:, at : at + half] = piece.astype(BF16)
    copies[4].wait()
    for side in range(2):
        piece = filters[:, side * half : (side + 1) * half].astype(BF16)
        at = (3 * side + 2) * half
        for copy in range(out.shape[0] // taps):
            out[copy * taps : (copy + 1) * taps, at : at + half] = piece


def spectra_kernel(scale, sent, first, first_t, turn, inner, inner_t, out):
    rows = out.shape[0]
    cols = out.shape[1] // 3
    half = cols // 2
    wc, ws = turn[:, :cols], turn[:, cols:]
    a = dot(first[...], sent[...])
    specs = []
    for j in range(3):
        at = [slice(j * half, (j + 1) * half), slice((3 + j) * half, (4 + j) * half)]
        re = jnp.concatenate([a[:rows, at[0]], a[:rows, at[1]]], axis=1)
        im = jnp.concatenate([a[rows:, at[0]], a[rows:, at[1]]], axis=1)
        b = jnp.concatenate([re * wc + im * ws, im * wc - re * ws], axis=1)
        f = dot(b.astype(BF16), inner[...])
        specs.append((f[:, :cols], f[:, cols:]))
    (xr, xi), (gr, gi), (hr, hi) = specs
    products = (
        (hr * xr - hi * xi, hr * xi + hi * xr, 1.0),
        (hr * gr + hi * gi, hr * gi - hi * gr, 1.0),
        (xr * gr + xi * gi, xr * gi - xi * gr, scale),
    )
    size = 1.0 / (rows * cols)
    for j, (pr, pi, factor) in enumerate(products):
        p = jnp.concatenate([pr, pi], axis=1).astype(BF16)
        u = dot(p, inner_t[...])
        ur, ui = u[:, :cols], u[:, cols:]
        v = jnp.concatenate([ur * wc - ui * ws, ur * ws + ui * wc], axis=0)
        y = dot(first_t[...], v.astype(BF16)) * (size * factor)
        for side in range(2):
            at = (3 * side + j) * half
            out[:, at : at + half] = y[:, side * half : (side + 1) * half].astype(BF16)


def finish_kernel(values, gate_in, cotangent, back, grad_values, grad_gate_in, grad_gate_out):
    half = back.shape[1] // 6
    for side in range(2):
        at = slice(side * half, (side + 1) * half)
        lo = 3 * side * half
        conv = back[:, lo : lo + half].astype(F32).T
        corr = back[:, lo + half : lo + 2 * half].astype(F32).T
        grad_values[at] = (gate_in[at].astype(F32) * corr).astype(BF16)
        grad_gate_in[at] = (values[at].astype(F32) * corr).astype(BF16)
        grad_gate_out[at] = (cotangent[at].astype(F32) * conv).astype(BF16)


def summed_over_batch(parts):
    order = [(i + BATCH_FIRST) % len(parts) for i in range(len(parts))]
    parts = jnp.concatenate([parts[BATCH_FIRST:], parts[:BATCH_FIRST]], axis=0)
    parts = lax.all_to_all(
        parts, "batch", split_axis=0, concat_axis=0, tiled=True, axis_index_groups=[order]
    )
    return parts.astype(F32).sum(axis=0)


def body(values, gate_in, gate_out, cotangent, filters):
    values, gate_in, gate_out, cotangent = (x[0] for x in (values, gate_in, gate_out, cotangent))
    cols, channels = values.shape
    shards = lax.axis_size("seq")
    replicas = lax.axis_size("batch")
    taps = filters.shape[0]
    wide = 3 * cols
    order = [SEQ_FIRST] + [i for i in range(shards) if i != SEQ_FIRST]
    first, first_t, turn, inner, inner_t = tables(shards, cols, order)
    scale = 1.0 / math.sqrt(channels * replicas // taps * shards * cols)

    def to_all(x):
        x = x.reshape(x.shape[0], 2, wide // 2)
        x = lax.all_to_all(
            x, "seq", split_axis=0, concat_axis=0, tiled=True, axis_index_groups=[order]
        )
        return x.reshape(x.shape[0], wide)

    pack = vmem_call(
        gather_kernel,
        jax.ShapeDtypeStruct((channels, wide), BF16),
        10 * channels * wide,
        12 * channels * wide,
        in_specs=[pl.BlockSpec(memory_space=pltpu.HBM)] * 5,
        scratch_shapes=[pltpu.VMEM((cols, channels), BF16)] * 4
        + [pltpu.VMEM((taps, cols), F32), pltpu.SemaphoreType.DMA((5,))],
    )
    sources = [
        pltpu.with_memory_space_constraint(x, pltpu.HBM)
        for x in (values, gate_in, cotangent, gate_out, filters)
    ]
    sent = to_all(pack(*sources))

    def spectra(*refs):
        spectra_kernel(scale, *refs)

    transform = vmem_call(
        spectra,
        jax.ShapeDtypeStruct((shards, wide), BF16),
        4 * shards * wide * (2 * cols + shards),
        4 * shards * wide,
    )
    back = to_all(transform(sent, first, first_t, turn, inner, inner_t))

    half = cols // 2
    terms = jnp.concatenate([back[:, wide // 2 - half : wide // 2], back[:, wide - half :]], axis=1)
    per_filter = terms.astype(F32).reshape(channels // taps, taps, cols).sum(axis=0)
    parts = per_filter.astype(BF16).reshape(replicas, taps // replicas, cols)
    finish = vmem_call(
        finish_kernel,
        [jax.ShapeDtypeStruct((cols, channels), BF16)] * 3,
        12 * cols * channels,
        20 * cols * channels,
    )
    grads = finish(values, gate_in, cotangent, back)
    grad_filters = summed_over_batch(parts)
    return tuple(x[None] for x in grads) + (grad_filters,)


def solution(mesh):
    placed = P(None, "seq", "batch")
    return jax.shard_map(
        body,
        mesh=mesh,
        in_specs=(placed, placed, placed, placed, P(None, "seq")),
        out_specs=(placed, placed, placed, P("batch", "seq")),
        check_vma=False,
    )
```

```python
import math

import jax
import jax.numpy as jnp
import ml_dtypes
import numpy as np
from jax import lax
from jax.experimental import pallas as pl
from jax.experimental.pallas import tpu as pltpu
from jax.sharding import PartitionSpec as P

F32 = jnp.float32
BF16 = jnp.bfloat16
VMEM_LIMIT = 12 << 20
SEQ_FIRST = 2 * 32 + 2 * 8 + 1 * 2
BATCH_FIRST = 2


def tables(rows, cols, order):
    theta = 2.0 * np.pi * np.outer(np.arange(rows) + 0.25, np.arange(rows)) / rows
    first = np.concatenate([np.cos(theta), -np.sin(theta)], 0)[:, order]
    phi = 2.0 * np.pi * np.outer(np.arange(rows) + 0.25, np.arange(cols)) / (rows * cols)
    turn = np.concatenate([np.cos(phi), np.sin(phi)], 1)
    angle = 2.0 * np.pi * (np.outer(np.arange(cols), np.arange(cols)) % cols) / cols
    c, s = np.cos(angle), np.sin(angle)
    inner = np.block([[c, -s], [s, c]])
    high = turn.astype(np.float32).astype(ml_dtypes.bfloat16).astype(np.float64)
    every = [first, first[:rows].T, first[rows:].T, inner, high, turn - high]
    return np.concatenate(every, 0).astype(np.float32).astype(ml_dtypes.bfloat16)


def dot(a, b):
    return jnp.dot(a, b, preferred_element_type=F32)


def vmem_call(kernel, out_shape, flops, size, **kwargs):
    return pl.pallas_call(
        kernel,
        out_shape=out_shape,
        compiler_params=pltpu.CompilerParams(vmem_limit_bytes=VMEM_LIMIT),
        cost_estimate=pl.CostEstimate(flops=flops, bytes_accessed=size, transcendentals=0),
        **kwargs,
    )


def gather_kernel(*refs):
    sources, out, held, sems = refs[:5], refs[5], refs[6:11], refs[11]
    copies = [pltpu.make_async_copy(s, h, sems.at[i]) for i, (s, h) in enumerate(zip(sources, held))]
    for copy in copies:
        copy.start()
    filters = held[4]
    half = out.shape[1] // 6
    taps = filters.shape[0]
    for part in range(2):
        a, b = held[2 * part : 2 * part + 2]
        copies[2 * part].wait()
        copies[2 * part + 1].wait()
        product = a[...].astype(F32) * b[...].astype(F32)
        for side in range(2):
            piece = product[side * half : (side + 1) * half].T
            at = (3 * side + part) * half
            out[:, at : at + half] = piece.astype(BF16)
    copies[4].wait()
    for side in range(2):
        piece = filters[:, side * half : (side + 1) * half].astype(BF16)
        at = (3 * side + 2) * half
        for copy in range(out.shape[0] // taps):
            out[copy * taps : (copy + 1) * taps, at : at + half] = piece


def spectra_kernel(scale, sent, mixing, out):
    shards = out.shape[0]
    wide = out.shape[1] // 2
    cols = wide // 3
    rows = 2 * shards
    inner = mixing[4 * rows : 4 * rows + 2 * cols]
    at = 4 * rows + 2 * cols
    turn = mixing[at : at + rows].astype(F32) + mixing[at + rows :].astype(F32)
    wc, ws = turn[:, :cols], turn[:, cols:]
    a = dot(mixing[: 2 * rows], jnp.concatenate([sent[:, :wide], sent[:, wide:]], axis=0))
    specs = []
    for j in range(3):
        at = slice(j * cols, (j + 1) * cols)
        re, im = a[:rows, at], a[rows:, at]
        b = jnp.concatenate([re * wc + im * ws, im * wc - re * ws], axis=1)
        f = dot(b.astype(BF16), inner)
        specs.append((f[:, :cols], f[:, cols:]))
    (xr, xi), (gr, gi), (hr, hi) = specs
    products = (
        (hr * xr - hi * xi, -hr * xi - hi * xr, 1.0),
        (hr * gr + hi * gi, hi * gr - hr * gi, 1.0),
        (xr * gr + xi * gi, xi * gr - xr * gi, scale),
    )
    for j, (pr, pi, factor) in enumerate(products):
        u = dot(jnp.concatenate([pr, pi], axis=1).astype(BF16), inner)
        ur, ui = u[:, :cols], u[:, cols:]
        vr, vi = ur * wc + ui * ws, ur * ws - ui * wc
        y = dot(mixing[2 * rows : 3 * rows], vr.astype(BF16))
        y = y + dot(mixing[3 * rows : 4 * rows], vi.astype(BF16))
        y = (y * (factor / (rows * cols))).astype(BF16)
        out[:, j * cols : (j + 1) * cols] = y[:shards]
        out[:, wide + j * cols : wide + (j + 1) * cols] = y[shards:]


def finish_kernel(values, gate_in, cotangent, back, parts, *outs):
    grad_values, grad_gate_in, grad_gate_out, grad_filters = outs
    half = back.shape[1] // 6
    for side in range(2):
        at = slice(side * half, (side + 1) * half)
        lo = 3 * side * half
        conv = back[:, lo : lo + half].astype(F32).T
        corr = back[:, lo + half : lo + 2 * half].astype(F32).T
        grad_values[at] = (gate_in[at].astype(F32) * corr).astype(BF16)
        grad_gate_in[at] = (values[at].astype(F32) * corr).astype(BF16)
        grad_gate_out[at] = (cotangent[at].astype(F32) * conv).astype(BF16)
    grad_filters[...] = parts[...].astype(F32).sum(axis=0)


def gathered_over_batch(parts):
    order = [(i + BATCH_FIRST) % len(parts) for i in range(len(parts))]
    parts = jnp.concatenate([parts[BATCH_FIRST:], parts[:BATCH_FIRST]], axis=0)
    return lax.all_to_all(
        parts, "batch", split_axis=0, concat_axis=0, tiled=True, axis_index_groups=[order]
    )


def body(values, gate_in, gate_out, cotangent, filters):
    values, gate_in, gate_out, cotangent = (x[0] for x in (values, gate_in, gate_out, cotangent))
    cols, channels = values.shape
    shards = lax.axis_size("seq")
    replicas = lax.axis_size("batch")
    taps = filters.shape[0]
    wide = 3 * cols
    order = [SEQ_FIRST] + [i for i in range(shards) if i != SEQ_FIRST]
    rows = [2 * i + side for side in range(2) for i in order]
    mixing = tables(2 * shards, cols // 2, rows)
    scale = 1.0 / math.sqrt(channels * replicas // taps * shards * cols)

    def to_all(x):
        x = x.reshape(x.shape[0], 2, wide // 2)
        x = lax.all_to_all(
            x, "seq", split_axis=0, concat_axis=0, tiled=True, axis_index_groups=[order]
        )
        return x.reshape(x.shape[0], wide)

    pack = vmem_call(
        gather_kernel,
        jax.ShapeDtypeStruct((channels, wide), BF16),
        10 * channels * wide,
        12 * channels * wide,
        in_specs=[pl.BlockSpec(memory_space=pltpu.HBM)] * 5,
        scratch_shapes=[pltpu.VMEM((cols, channels), BF16)] * 4
        + [pltpu.VMEM((taps, cols), F32), pltpu.SemaphoreType.DMA((5,))],
    )
    sources = [
        pltpu.with_memory_space_constraint(x, pltpu.HBM)
        for x in (values, gate_in, cotangent, gate_out, filters)
    ]
    sent = to_all(pack(*sources))

    def spectra(*refs):
        spectra_kernel(scale, *refs)

    transform = vmem_call(
        spectra,
        jax.ShapeDtypeStruct((shards, wide), BF16),
        2 * shards * wide * (2 * cols + 4 * shards),
        4 * shards * wide,
    )
    back = to_all(transform(sent, mixing))

    half = cols // 2
    terms = jnp.concatenate([back[:, wide // 2 - half : wide // 2], back[:, wide - half :]], axis=1)
    per_filter = terms.astype(F32).reshape(channels // taps, taps, cols).sum(axis=0)
    parts = per_filter.astype(BF16).reshape(replicas, taps // replicas, cols)
    finish = vmem_call(
        finish_kernel,
        [jax.ShapeDtypeStruct((cols, channels), BF16)] * 3
        + [jax.ShapeDtypeStruct((taps // replicas, cols), F32)],
        12 * cols * channels,
        20 * cols * channels,
    )
    *grads, grad_filters = finish(values, gate_in, cotangent, back, gathered_over_batch(parts))
    return tuple(x[None] for x in grads) + (grad_filters,)


def solution(mesh):
    placed = P(None, "seq", "batch")
    return jax.shard_map(
        body,
        mesh=mesh,
        in_specs=(placed, placed, placed, placed, P(None, "seq")),
        out_specs=(placed, placed, placed, P("batch", "seq")),
        check_vma=False,
    )
```

```python
import functools
import math

import jax
import jax.numpy as jnp
import ml_dtypes
import numpy as np
from jax import lax
from jax.experimental import pallas as pl
from jax.experimental.pallas import tpu as pltpu
from jax.sharding import PartitionSpec as P

F32 = jnp.float32
BF16 = jnp.bfloat16
VMEM_LIMIT = 12 << 20
SEQ_FIRST = 2 * 32 + 2 * 8 + 2 * 2 + 1
BATCH_FIRST = 2


def tables(rows, cols, order):
    theta = 2.0 * np.pi * np.outer(np.arange(rows) + 0.25, np.arange(rows)) / rows
    first = np.concatenate([np.cos(theta), -np.sin(theta)], 0)[:, order]
    phi = 2.0 * np.pi * np.outer(np.arange(rows) + 0.25, np.arange(cols)) / (rows * cols)
    turn = np.concatenate([np.cos(phi), np.sin(phi)], 1)
    angle = 2.0 * np.pi * (np.outer(np.arange(cols), np.arange(cols)) % cols) / cols
    c, s = np.cos(angle), np.sin(angle)
    inner = np.block([[c, -s], [s, c]])
    high = turn.astype(np.float32).astype(ml_dtypes.bfloat16).astype(np.float64)
    back = first.T / (rows * cols)
    groups = [first, inner], [back[:, :rows], back[:, rows:], high, turn - high]
    return [np.concatenate(g, 0).astype(np.float32).astype(ml_dtypes.bfloat16) for g in groups]


def dot(a, b):
    return jnp.dot(a, b, preferred_element_type=F32)


def vmem_call(kernel, out_shape, flops, size, flags=None, **kwargs):
    return pl.pallas_call(
        kernel,
        out_shape=out_shape,
        compiler_params=pltpu.CompilerParams(vmem_limit_bytes=VMEM_LIMIT, flags=flags),
        cost_estimate=pl.CostEstimate(flops=flops, bytes_accessed=size, transcendentals=0),
        **kwargs,
    )


def gather_kernel(*refs):
    sources, out, held, sems = refs[:5], refs[5], refs[6:11], refs[11]
    copies = [pltpu.make_async_copy(s, h, sems.at[i]) for i, (s, h) in enumerate(zip(sources, held))]
    for copy in copies:
        copy.start()
    filters = held[4]
    half = out.shape[1] // 6
    taps = filters.shape[0]
    for part in range(2):
        a, b = held[2 * part : 2 * part + 2]
        copies[2 * part].wait()
        copies[2 * part + 1].wait()
        product = a[...].astype(F32) * b[...].astype(F32)
        for side in range(2):
            piece = product[side * half : (side + 1) * half].T
            at = (3 * side + part) * half
            out[:, at : at + half] = piece.astype(BF16)
    copies[4].wait()
    for side in range(2):
        piece = filters[:, side * half : (side + 1) * half].astype(BF16)
        at = (3 * side + 2) * half
        for copy in range(out.shape[0] // taps):
            out[copy * taps : (copy + 1) * taps, at : at + half] = piece


def spectra_kernel(sent, early, late, out):
    shards = out.shape[0]
    wide = out.shape[1] // 2
    cols = wide // 3
    rows = 2 * shards
    mixing, inner = early[: 2 * rows], early[2 * rows :]
    series = jnp.concatenate([sent[:, :wide], sent[:, wide:]], axis=0)
    turn = late[2 * rows : 3 * rows].astype(F32) + late[3 * rows :].astype(F32)
    wc, ws = turn[:, :cols], turn[:, cols:]

    def forward(re, im):
        b = jnp.concatenate([re * wc + im * ws, im * wc - re * ws], axis=1)
        f = dot(b.astype(BF16), inner)
        return f[:, :cols], f[:, cols:]

    def inverse(pr, pi):
        u = dot(jnp.concatenate([pr, pi], axis=1).astype(BF16), inner)
        ur, ui = u[:, :cols], u[:, cols:]
        return (ur * wc + ui * ws).astype(BF16), (ur * ws - ui * wc).astype(BF16)

    def last(vr, vi):
        y = dot(late[:rows], vr) + dot(late[rows : 2 * rows], vi)
        return y.astype(BF16)

    def put(y, at):
        out[:, at : at + y.shape[1]] = y[:shards]
        out[:, wide + at : wide + at + y.shape[1]] = y[shards:]

    a = dot(mixing, series[:, : 2 * cols])
    c = dot(mixing, series[:, 2 * cols :])
    xr, xi = forward(a[:rows, :cols], a[rows:, :cols])
    gr, gi = forward(a[:rows, cols:], a[rows:, cols:])
    hr, hi = forward(c[:rows], c[rows:])
    v2 = inverse(xr * gr + xi * gi, xi * gr - xr * gi)
    v0 = inverse(hr * xr - hi * xi, -hr * xi - hi * xr)
    put(last(jnp.concatenate([v0[0], v2[0]], 1), jnp.concatenate([v0[1], v2[1]], 1))[:, :cols], 0)
    v1 = inverse(hr * gr + hi * gi, hi * gr - hr * gi)
    put(last(jnp.concatenate([v1[0], v2[0]], 1), jnp.concatenate([v1[1], v2[1]], 1)), cols)


def finish_kernel(scale, values, gate_in, cotangent, back, parts, *outs):
    grad_values, grad_gate_in, grad_gate_out, grad_filters = outs
    half = back.shape[1] // 6
    for side in range(2):
        at = slice(side * half, (side + 1) * half)
        lo = 3 * side * half
        conv = back[:, lo : lo + half].astype(F32).T
        corr = back[:, lo + half : lo + 2 * half].astype(F32).T
        grad_values[at] = (gate_in[at].astype(F32) * corr).astype(BF16)
        grad_gate_in[at] = (values[at].astype(F32) * corr).astype(BF16)
        grad_gate_out[at] = (cotangent[at].astype(F32) * conv).astype(BF16)
    grad_filters[...] = parts[...].astype(F32).sum(axis=0) * scale


def gathered_over_batch(parts):
    order = [(i + BATCH_FIRST) % len(parts) for i in range(len(parts))]
    parts = jnp.concatenate([parts[BATCH_FIRST:], parts[:BATCH_FIRST]], axis=0)
    return lax.all_to_all(
        parts, "batch", split_axis=0, concat_axis=0, tiled=True, axis_index_groups=[order]
    )


def body(values, gate_in, gate_out, cotangent, filters):
    values, gate_in, gate_out, cotangent = (x[0] for x in (values, gate_in, gate_out, cotangent))
    cols, channels = values.shape
    shards = lax.axis_size("seq")
    replicas = lax.axis_size("batch")
    taps = filters.shape[0]
    wide = 3 * cols
    order = sorted(range(shards), key=lambda i: (i != SEQ_FIRST, 1 - i % 2, i))
    rows = [2 * i + side for side in range(2) for i in order]
    early, late = tables(2 * shards, cols // 2, rows)
    scale = 1.0 / math.sqrt(channels * replicas // taps * shards * cols)

    def to_all(x):
        x = x.reshape(x.shape[0], 2, wide // 2)
        x = lax.all_to_all(
            x, "seq", split_axis=0, concat_axis=0, tiled=True, axis_index_groups=[order]
        )
        return x.reshape(x.shape[0], wide)

    pack = vmem_call(
        gather_kernel,
        jax.ShapeDtypeStruct((channels, wide), BF16),
        10 * channels * wide,
        12 * channels * wide,
        in_specs=[pl.BlockSpec(memory_space=pltpu.HBM)] * 5,
        scratch_shapes=[pltpu.VMEM((cols, channels), BF16)] * 4
        + [pltpu.VMEM((taps, cols), F32), pltpu.SemaphoreType.DMA((5,))],
    )
    sources = [
        pltpu.with_memory_space_constraint(x, pltpu.HBM)
        for x in (values, gate_in, cotangent, gate_out, filters)
    ]
    sent = to_all(pack(*sources))

    transform = vmem_call(
        spectra_kernel,
        jax.ShapeDtypeStruct((shards, wide), BF16),
        2 * shards * wide * (2 * cols + 4 * shards),
        4 * shards * wide,
    )
    back = to_all(transform(sent, early, late))

    half = cols // 2
    terms = jnp.concatenate([back[:, wide // 2 - half : wide // 2], back[:, wide - half :]], axis=1)
    per_filter = terms.astype(F32).reshape(channels // taps, taps, cols).sum(axis=0)
    parts = per_filter.astype(BF16).reshape(replicas, taps // replicas, cols)
    finish = vmem_call(
        functools.partial(finish_kernel, scale),
        [jax.ShapeDtypeStruct((cols, channels), BF16)] * 3
        + [jax.ShapeDtypeStruct((taps // replicas, cols), F32)],
        12 * cols * channels,
        20 * cols * channels,
    )
    *grads, grad_filters = finish(values, gate_in, cotangent, back, gathered_over_batch(parts))
    return tuple(x[None] for x in grads) + (grad_filters,)


def solution(mesh):
    placed = P(None, "seq", "batch")
    return jax.shard_map(
        body,
        mesh=mesh,
        in_specs=(placed, placed, placed, placed, P(None, "seq")),
        out_specs=(placed, placed, placed, P("batch", "seq")),
        check_vma=False,
    )
```

```python
import functools
import math

import jax
import jax.numpy as jnp
import ml_dtypes
import numpy as np
from jax import lax
from jax.experimental import pallas as pl
from jax.experimental.pallas import tpu as pltpu
from jax.sharding import PartitionSpec as P

F32 = jnp.float32
BF16 = jnp.bfloat16
VMEM_LIMIT = 12 << 20
SEQ_FIRST = 2 * 32 + 2 * 8 + 2 * 2 + 1
BATCH_FIRST = 2


def tables(rows, cols, order):
    theta = 2.0 * np.pi * np.outer(np.arange(rows) + 0.25, np.arange(rows)) / rows
    first = np.concatenate([np.cos(theta), -np.sin(theta)], 0)[:, order]
    phi = 2.0 * np.pi * np.outer(np.arange(rows) + 0.25, np.arange(cols)) / (rows * cols)
    turn = np.concatenate([np.cos(phi), np.sin(phi)], 1)
    angle = 2.0 * np.pi * (np.outer(np.arange(cols), np.arange(cols)) % cols) / cols
    c, s = np.cos(angle), np.sin(angle)
    inner = np.block([[c, -s], [s, c]])
    high = turn.astype(np.float32).astype(ml_dtypes.bfloat16).astype(np.float64)
    back = first.T / (rows * cols)
    groups = [first, inner], [back[:, :rows], back[:, rows:], high, turn - high]
    return [np.concatenate(g, 0).astype(np.float32).astype(ml_dtypes.bfloat16) for g in groups]


def dot(a, b):
    return jnp.dot(a, b, preferred_element_type=F32)


def vmem_call(kernel, out_shape, flops, size, flags=None, **kwargs):
    return pl.pallas_call(
        kernel,
        out_shape=out_shape,
        compiler_params=pltpu.CompilerParams(vmem_limit_bytes=VMEM_LIMIT, flags=flags),
        cost_estimate=pl.CostEstimate(flops=flops, bytes_accessed=size, transcendentals=0),
        **kwargs,
    )


def gather_kernel(*refs):
    sources, out, held, sems = refs[:5], refs[5], refs[6:11], refs[11]
    copies = [pltpu.make_async_copy(s, h, sems.at[i]) for i, (s, h) in enumerate(zip(sources, held))]
    for copy in copies:
        copy.start()
    filters = held[4]
    half = out.shape[1] // 6
    taps = filters.shape[0]
    for part in range(2):
        a, b = held[2 * part : 2 * part + 2]
        copies[2 * part].wait()
        copies[2 * part + 1].wait()
        product = (a[...].astype(F32) * b[...].astype(F32)).astype(BF16)
        for side in range(2):
            at = (3 * side + part) * half
            out[:, at : at + half] = product[side * half : (side + 1) * half].T
    copies[4].wait()
    for side in range(2):
        piece = filters[:, side * half : (side + 1) * half].astype(BF16)
        at = (3 * side + 2) * half
        for copy in range(out.shape[0] // taps):
            out[copy * taps : (copy + 1) * taps, at : at + half] = piece


def spectra_kernel(sent, early, late, out):
    shards = out.shape[0]
    wide = out.shape[1] // 2
    cols = wide // 3
    rows = 2 * shards
    mixing, inner = early[: 2 * rows], early[2 * rows :]
    series = jnp.concatenate([sent[:, :wide], sent[:, wide:]], axis=0)
    turn = late[2 * rows : 3 * rows].astype(F32) + late[3 * rows :].astype(F32)
    wc, ws = turn[:, :cols], turn[:, cols:]

    def forward(re, im):
        b = jnp.concatenate([re * wc + im * ws, im * wc - re * ws], axis=1)
        f = dot(b.astype(BF16), inner)
        return f[:, :cols], f[:, cols:]

    def inverse(pr, pi):
        u = dot(jnp.concatenate([pr, pi], axis=1).astype(BF16), inner)
        ur, ui = u[:, :cols], u[:, cols:]
        return (ur * wc + ui * ws).astype(BF16), (ur * ws - ui * wc).astype(BF16)

    def last(vr, vi):
        y = dot(late[:rows], vr) + dot(late[rows : 2 * rows], vi)
        return y.astype(BF16)

    def put(y, at):
        out[:, at : at + y.shape[1]] = y[:shards]
        out[:, wide + at : wide + at + y.shape[1]] = y[shards:]

    a = dot(mixing, series[:, : 2 * cols])
    c = dot(mixing, series[:, 2 * cols :])
    xr, xi = forward(a[:rows, :cols], a[rows:, :cols])
    gr, gi = forward(a[:rows, cols:], a[rows:, cols:])
    hr, hi = forward(c[:rows], c[rows:])
    v0 = inverse(hr * xr - hi * xi, -hr * xi - hi * xr)
    v2 = inverse(xr * gr + xi * gi, xi * gr - xr * gi)
    put(last(jnp.concatenate([v0[0], v2[0]], 1), jnp.concatenate([v0[1], v2[1]], 1))[:, :cols], 0)
    v1 = inverse(hr * gr + hi * gi, hi * gr - hr * gi)
    put(last(jnp.concatenate([v1[0], v2[0]], 1), jnp.concatenate([v1[1], v2[1]], 1)), cols)


def finish_kernel(scale, values, gate_in, cotangent, back, parts, *outs):
    grad_values, grad_gate_in, grad_gate_out, grad_filters = outs
    half = back.shape[1] // 6
    for side in range(2):
        at = slice(side * half, (side + 1) * half)
        lo = 3 * side * half
        conv = back[:, lo : lo + half].T.astype(F32)
        corr = back[:, lo + half : lo + 2 * half].T.astype(F32)
        grad_values[at] = (gate_in[at].astype(F32) * corr).astype(BF16)
        grad_gate_in[at] = (values[at].astype(F32) * corr).astype(BF16)
        grad_gate_out[at] = (cotangent[at].astype(F32) * conv).astype(BF16)
    grad_filters[...] = parts[...].astype(F32).sum(axis=0) * scale


def gathered_over_batch(parts):
    order = [(i + BATCH_FIRST) % len(parts) for i in range(len(parts))]
    parts = jnp.concatenate([parts[BATCH_FIRST:], parts[:BATCH_FIRST]], axis=0)
    return lax.all_to_all(
        parts, "batch", split_axis=0, concat_axis=0, tiled=True, axis_index_groups=[order]
    )


def body(values, gate_in, gate_out, cotangent, filters):
    values, gate_in, gate_out, cotangent = (x[0] for x in (values, gate_in, gate_out, cotangent))
    cols, channels = values.shape
    shards = lax.axis_size("seq")
    replicas = lax.axis_size("batch")
    taps = filters.shape[0]
    wide = 3 * cols
    order = sorted(range(shards), key=lambda i: (i != SEQ_FIRST, 1 - i % 2, i))
    rows = [2 * i + side for side in range(2) for i in order]
    early, late = tables(2 * shards, cols // 2, rows)
    scale = 1.0 / math.sqrt(channels * replicas // taps * shards * cols)

    def to_all(x):
        x = x.reshape(x.shape[0], 2, wide // 2)
        x = lax.all_to_all(
            x, "seq", split_axis=0, concat_axis=0, tiled=True, axis_index_groups=[order]
        )
        return x.reshape(x.shape[0], wide)

    pack = vmem_call(
        gather_kernel,
        jax.ShapeDtypeStruct((channels, wide), BF16),
        10 * channels * wide,
        12 * channels * wide,
        in_specs=[pl.BlockSpec(memory_space=pltpu.HBM)] * 5,
        scratch_shapes=[pltpu.VMEM((cols, channels), BF16)] * 4
        + [pltpu.VMEM((taps, cols), F32), pltpu.SemaphoreType.DMA((5,))],
    )
    sources = [
        pltpu.with_memory_space_constraint(x, pltpu.HBM)
        for x in (values, gate_in, cotangent, gate_out, filters)
    ]
    sent = to_all(pack(*sources))

    transform = vmem_call(
        spectra_kernel,
        jax.ShapeDtypeStruct((shards, wide), BF16),
        2 * shards * wide * (2 * cols + 4 * shards),
        4 * shards * wide,
    )
    back = to_all(transform(sent, early, late))

    half = cols // 2
    terms = jnp.concatenate([back[:, wide // 2 - half : wide // 2], back[:, wide - half :]], axis=1)
    per_filter = terms.astype(F32).reshape(channels // taps, taps, cols).sum(axis=0)
    parts = per_filter.astype(BF16).reshape(replicas, taps // replicas, cols)
    finish = vmem_call(
        functools.partial(finish_kernel, scale),
        [jax.ShapeDtypeStruct((cols, channels), BF16)] * 3
        + [jax.ShapeDtypeStruct((taps // replicas, cols), F32)],
        12 * cols * channels,
        20 * cols * channels,
    )
    *grads, grad_filters = finish(values, gate_in, cotangent, back, gathered_over_batch(parts))
    return tuple(x[None] for x in grads) + (grad_filters,)


def solution(mesh):
    placed = P(None, "seq", "batch")
    return jax.shard_map(
        body,
        mesh=mesh,
        in_specs=(placed, placed, placed, placed, P(None, "seq")),
        out_specs=(placed, placed, placed, P("batch", "seq")),
        check_vma=False,
    )
```

```python
import functools
import math

import jax
import jax.numpy as jnp
import ml_dtypes
import numpy as np
from jax import lax
from jax.experimental import pallas as pl
from jax.experimental.pallas import tpu as pltpu
from jax.sharding import PartitionSpec as P

F32 = jnp.float32
BF16 = jnp.bfloat16
VMEM_LIMIT = 12 << 20
SEQ_FIRST = 2 * 32 + 2 * 8 + 2 * 2 + 1
BATCH_FIRST = 2


def tables(rows, cols, order):
    theta = 2.0 * np.pi * np.outer(np.arange(rows) + 0.25, np.arange(rows)) / rows
    first = np.concatenate([np.cos(theta), -np.sin(theta)], 0)[:, order]
    phi = 2.0 * np.pi * np.outer(np.arange(rows) + 0.25, np.arange(cols)) / (rows * cols)
    turn = np.concatenate([np.cos(phi), np.sin(phi)], 1)
    angle = 2.0 * np.pi * (np.outer(np.arange(cols), np.arange(cols)) % cols) / cols
    c, s = np.cos(angle), np.sin(angle)
    inner = np.block([[c, -s], [s, c]])
    high = turn.astype(np.float32).astype(ml_dtypes.bfloat16).astype(np.float64)
    back = first.T / (rows * cols)
    groups = [first, inner], [back[:, :rows], back[:, rows:], high, turn - high]
    return [np.concatenate(g, 0).astype(np.float32).astype(ml_dtypes.bfloat16) for g in groups]


def dot(a, b):
    return jnp.dot(a, b, preferred_element_type=F32)


def vmem_call(kernel, out_shape, flops, size, flags=None, **kwargs):
    return pl.pallas_call(
        kernel,
        out_shape=out_shape,
        compiler_params=pltpu.CompilerParams(vmem_limit_bytes=VMEM_LIMIT, flags=flags),
        cost_estimate=pl.CostEstimate(flops=flops, bytes_accessed=size, transcendentals=0),
        **kwargs,
    )


def gather_kernel(*refs):
    sources, out, held, sems = refs[:5], refs[5], refs[6:11], refs[11]
    copies = [pltpu.make_async_copy(s, h, sems.at[i]) for i, (s, h) in enumerate(zip(sources, held))]
    for copy in copies:
        copy.start()
    filters = held[4]
    half = out.shape[1] // 6
    taps = filters.shape[0]
    for part in range(2):
        a, b = held[2 * part : 2 * part + 2]
        copies[2 * part].wait()
        copies[2 * part + 1].wait()
        product = (a[...].astype(F32) * b[...].astype(F32)).astype(BF16)
        for side in range(2):
            at = (3 * side + part) * half
            out[:, at : at + half] = product[side * half : (side + 1) * half].T
    copies[4].wait()
    for side in range(2):
        piece = filters[:, side * half : (side + 1) * half].astype(BF16)
        at = (3 * side + 2) * half
        for copy in range(out.shape[0] // taps):
            out[copy * taps : (copy + 1) * taps, at : at + half] = piece


def spectra_kernel(sent, early, late, out):
    shards = out.shape[0]
    wide = out.shape[1] // 2
    cols = wide // 3
    rows = 2 * shards
    mixing, inner = early[: 2 * rows], early[2 * rows :]
    series = jnp.concatenate([sent[:, :wide], sent[:, wide:]], axis=0)
    turn = late[2 * rows : 3 * rows].astype(F32) + late[3 * rows :].astype(F32)
    wc, ws = turn[:, :cols], turn[:, cols:]

    def forward(re, im):
        b = jnp.concatenate([re * wc + im * ws, im * wc - re * ws], axis=1)
        f = dot(b.astype(BF16), inner)
        return f[:, :cols], f[:, cols:]

    def inverse(pr, pi):
        u = dot(jnp.concatenate([pr, pi], axis=1).astype(BF16), inner)
        ur, ui = u[:, :cols], u[:, cols:]
        return (ur * wc + ui * ws).astype(BF16), (ur * ws - ui * wc).astype(BF16)

    def last(vr, vi):
        y = dot(late[:rows], vr) + dot(late[rows : 2 * rows], vi)
        return y.astype(BF16)

    def put(y, at):
        out[:, at : at + y.shape[1]] = y[:shards]
        out[:, wide + at : wide + at + y.shape[1]] = y[shards:]

    a = dot(mixing, series[:, : 2 * cols])
    c = dot(mixing, series[:, 2 * cols :])
    xr, xi = forward(a[:rows, :cols], a[rows:, :cols])
    gr, gi = forward(a[:rows, cols:], a[rows:, cols:])
    hr, hi = forward(c[:rows], c[rows:])
    v0 = inverse(hr * xr - hi * xi, -hr * xi - hi * xr)
    v2 = inverse(xr * gr + xi * gi, xi * gr - xr * gi)
    put(last(jnp.concatenate([v0[0], v2[0]], 1), jnp.concatenate([v0[1], v2[1]], 1))[:, :cols], 0)
    v1 = inverse(hr * gr + hi * gi, hi * gr - hr * gi)
    put(last(jnp.concatenate([v1[0], v2[0]], 1), jnp.concatenate([v1[1], v2[1]], 1)), cols)


def finish_kernel(scale, values, gate_in, cotangent, back, parts, *outs):
    grad_values, grad_gate_in, grad_gate_out, grad_filters = outs
    half = back.shape[1] // 6
    for side in range(2):
        at = slice(side * half, (side + 1) * half)
        lo = 3 * side * half
        conv = back[:, lo : lo + half].T.astype(F32)
        corr = back[:, lo + half : lo + 2 * half].T.astype(F32)
        grad_values[at] = (gate_in[at].astype(F32) * corr).astype(BF16)
        grad_gate_in[at] = (values[at].astype(F32) * corr).astype(BF16)
        grad_gate_out[at] = (cotangent[at].astype(F32) * conv).astype(BF16)
    grad_filters[...] = parts[...].astype(F32).sum(axis=0) * scale


def gathered_over_batch(parts):
    order = [(i + BATCH_FIRST) % len(parts) for i in range(len(parts))]
    parts = jnp.concatenate([parts[BATCH_FIRST:], parts[:BATCH_FIRST]], axis=0)
    return lax.all_to_all(
        parts, "batch", split_axis=0, concat_axis=0, tiled=True, axis_index_groups=[order]
    )


def body(values, gate_in, gate_out, cotangent, filters):
    values, gate_in, gate_out, cotangent = (x[0] for x in (values, gate_in, gate_out, cotangent))
    cols, channels = values.shape
    shards = lax.axis_size("seq")
    replicas = lax.axis_size("batch")
    taps = filters.shape[0]
    wide = 3 * cols
    order = sorted(range(shards), key=lambda i: (i != SEQ_FIRST, 1 - i % 2, -(i & 6), i))
    rows = [2 * i + side for side in range(2) for i in order]
    early, late = tables(2 * shards, cols // 2, rows)
    scale = 1.0 / math.sqrt(channels * replicas // taps * shards * cols)

    def to_all(x):
        x = x.reshape(x.shape[0], 2, wide // 2)
        x = lax.all_to_all(
            x, "seq", split_axis=0, concat_axis=0, tiled=True, axis_index_groups=[order]
        )
        return x.reshape(x.shape[0], wide)

    pack = vmem_call(
        gather_kernel,
        jax.ShapeDtypeStruct((channels, wide), BF16),
        10 * channels * wide,
        12 * channels * wide,
        in_specs=[pl.BlockSpec(memory_space=pltpu.HBM)] * 5,
        scratch_shapes=[pltpu.VMEM((cols, channels), BF16)] * 4
        + [pltpu.VMEM((taps, cols), F32), pltpu.SemaphoreType.DMA((5,))],
    )
    sources = [
        pltpu.with_memory_space_constraint(x, pltpu.HBM)
        for x in (values, gate_in, cotangent, gate_out, filters)
    ]
    sent = to_all(pack(*sources))

    transform = vmem_call(
        spectra_kernel,
        jax.ShapeDtypeStruct((shards, wide), BF16),
        2 * shards * wide * (2 * cols + 4 * shards),
        4 * shards * wide,
    )
    back = to_all(transform(sent, early, late))

    half = cols // 2
    terms = jnp.concatenate([back[:, wide // 2 - half : wide // 2], back[:, wide - half :]], axis=1)
    per_filter = terms.astype(F32).reshape(channels // taps, taps, cols).sum(axis=0)
    parts = per_filter.astype(BF16).reshape(replicas, taps // replicas, cols)
    finish = vmem_call(
        functools.partial(finish_kernel, scale),
        [jax.ShapeDtypeStruct((cols, channels), BF16)] * 3
        + [jax.ShapeDtypeStruct((taps // replicas, cols), F32)],
        12 * cols * channels,
        20 * cols * channels,
    )
    *grads, grad_filters = finish(values, gate_in, cotangent, back, gathered_over_batch(parts))
    return tuple(x[None] for x in grads) + (grad_filters,)


def solution(mesh):
    placed = P(None, "seq", "batch")
    return jax.shard_map(
        body,
        mesh=mesh,
        in_specs=(placed, placed, placed, placed, P(None, "seq")),
        out_specs=(placed, placed, placed, P("batch", "seq")),
        check_vma=False,
    )
```

```python
import functools
import math

import jax
import jax.numpy as jnp
import ml_dtypes
import numpy as np
from jax import lax
from jax.experimental import pallas as pl
from jax.experimental.pallas import tpu as pltpu
from jax.sharding import PartitionSpec as P

F32 = jnp.float32
BF16 = jnp.bfloat16
VMEM_LIMIT = 12 << 20
SEQ_FIRST = 2 * 32 + 2 * 8 + 2 * 2 + 1
BATCH_FIRST = 2


def tables(rows, cols, order):
    theta = 2.0 * np.pi * np.outer(np.arange(rows) + 0.25, np.arange(rows)) / rows
    first = np.concatenate([np.cos(theta), -np.sin(theta)], 0)[:, order]
    phi = 2.0 * np.pi * np.outer(np.arange(rows) + 0.25, np.arange(cols)) / (rows * cols)
    turn = np.concatenate([np.cos(phi), np.sin(phi)], 1)
    angle = 2.0 * np.pi * (np.outer(np.arange(cols), np.arange(cols)) % cols) / cols
    c, s = np.cos(angle), np.sin(angle)
    inner = np.block([[c, -s], [s, c]])
    high = turn.astype(np.float32).astype(ml_dtypes.bfloat16).astype(np.float64)
    back = first.T / (rows * cols)
    groups = [first, inner], [back[:, :rows], back[:, rows:], high, turn - high]
    return [np.concatenate(g, 0).astype(np.float32).astype(ml_dtypes.bfloat16) for g in groups]


def dot(a, b):
    return jnp.dot(a, b, preferred_element_type=F32)


def vmem_call(kernel, out_shape, flops, size, flags=None, **kwargs):
    return pl.pallas_call(
        kernel,
        out_shape=out_shape,
        compiler_params=pltpu.CompilerParams(vmem_limit_bytes=VMEM_LIMIT, flags=flags),
        cost_estimate=pl.CostEstimate(flops=flops, bytes_accessed=size, transcendentals=0),
        **kwargs,
    )


def gather_kernel(*refs):
    sources, out, held, sems = refs[:5], refs[5], refs[6:11], refs[11]
    copies = [pltpu.make_async_copy(s, h, sems.at[i]) for i, (s, h) in enumerate(zip(sources, held))]
    for i in (0, 1, 4, 2, 3):
        copies[i].start()
    filters = held[4]
    half = out.shape[1] // 6
    taps = filters.shape[0]
    for part in range(2):
        if part:
            copies[4].wait()
            for side in range(2):
                piece = filters[:, side * half : (side + 1) * half].astype(BF16)
                at = (3 * side + 2) * half
                for copy in range(out.shape[0] // taps):
                    out[copy * taps : (copy + 1) * taps, at : at + half] = piece
        a, b = held[2 * part : 2 * part + 2]
        copies[2 * part].wait()
        copies[2 * part + 1].wait()
        product = (a[...].astype(F32) * b[...].astype(F32)).astype(BF16)
        for side in range(2):
            at = (3 * side + part) * half
            out[:, at : at + half] = product[side * half : (side + 1) * half].T


def spectra_kernel(sent, early, late, out):
    shards = out.shape[0]
    wide = out.shape[1] // 2
    cols = wide // 3
    rows = 2 * shards
    mixing, inner = early[: 2 * rows], early[2 * rows :]
    series = jnp.concatenate([sent[:, :wide], sent[:, wide:]], axis=0)
    turn = late[2 * rows : 3 * rows].astype(F32) + late[3 * rows :].astype(F32)
    wc, ws = turn[:, :cols], turn[:, cols:]

    def forward(re, im):
        b = jnp.concatenate([re * wc + im * ws, im * wc - re * ws], axis=1)
        f = dot(b.astype(BF16), inner)
        return f[:, :cols], f[:, cols:]

    def inverse(pr, pi):
        u = dot(jnp.concatenate([pr, pi], axis=1).astype(BF16), inner)
        ur, ui = u[:, :cols], u[:, cols:]
        return (ur * wc + ui * ws).astype(BF16), (ur * ws - ui * wc).astype(BF16)

    def last(vr, vi):
        y = dot(late[:rows], vr) + dot(late[rows : 2 * rows], vi)
        return y.astype(BF16)

    def put(y, at):
        out[:, at : at + y.shape[1]] = y[:shards]
        out[:, wide + at : wide + at + y.shape[1]] = y[shards:]

    a = dot(mixing, series[:, : 2 * cols])
    c = dot(mixing, series[:, 2 * cols :])
    xr, xi = forward(a[:rows, :cols], a[rows:, :cols])
    gr, gi = forward(a[:rows, cols:], a[rows:, cols:])
    hr, hi = forward(c[:rows], c[rows:])
    v0 = inverse(hr * xr - hi * xi, -hr * xi - hi * xr)
    v2 = inverse(xr * gr + xi * gi, xi * gr - xr * gi)
    put(last(jnp.concatenate([v0[0], v2[0]], 1), jnp.concatenate([v0[1], v2[1]], 1))[:, :cols], 0)
    v1 = inverse(hr * gr + hi * gi, hi * gr - hr * gi)
    put(last(jnp.concatenate([v1[0], v2[0]], 1), jnp.concatenate([v1[1], v2[1]], 1)), cols)


def finish_kernel(scale, values, gate_in, cotangent, back, parts, *outs):
    grad_values, grad_gate_in, grad_gate_out, grad_filters = outs
    half = back.shape[1] // 6
    for side in range(2):
        at = slice(side * half, (side + 1) * half)
        lo = 3 * side * half
        conv = back[:, lo : lo + half].T.astype(F32)
        corr = back[:, lo + half : lo + 2 * half].T.astype(F32)
        grad_values[at] = (gate_in[at].astype(F32) * corr).astype(BF16)
        grad_gate_in[at] = (values[at].astype(F32) * corr).astype(BF16)
        grad_gate_out[at] = (cotangent[at].astype(F32) * conv).astype(BF16)
    grad_filters[...] = parts[...].astype(F32).sum(axis=0) * scale


def gathered_over_batch(parts):
    order = [(i + BATCH_FIRST) % len(parts) for i in range(len(parts))]
    parts = jnp.concatenate([parts[BATCH_FIRST:], parts[:BATCH_FIRST]], axis=0)
    return lax.all_to_all(
        parts, "batch", split_axis=0, concat_axis=0, tiled=True, axis_index_groups=[order]
    )


def body(values, gate_in, gate_out, cotangent, filters):
    values, gate_in, gate_out, cotangent = (x[0] for x in (values, gate_in, gate_out, cotangent))
    cols, channels = values.shape
    shards = lax.axis_size("seq")
    replicas = lax.axis_size("batch")
    taps = filters.shape[0]
    wide = 3 * cols
    order = sorted(range(shards), key=lambda i: (i != SEQ_FIRST, 1 - i % 2, -(i & 6), i))
    rows = [2 * i + side for side in range(2) for i in order]
    early, late = tables(2 * shards, cols // 2, rows)
    scale = 1.0 / math.sqrt(channels * replicas // taps * shards * cols)

    def to_all(x):
        x = x.reshape(x.shape[0], 2, wide // 2)
        x = lax.all_to_all(
            x, "seq", split_axis=0, concat_axis=0, tiled=True, axis_index_groups=[order]
        )
        return x.reshape(x.shape[0], wide)

    pack = vmem_call(
        gather_kernel,
        jax.ShapeDtypeStruct((channels, wide), BF16),
        10 * channels * wide,
        12 * channels * wide,
        in_specs=[pl.BlockSpec(memory_space=pltpu.HBM)] * 5,
        scratch_shapes=[pltpu.VMEM((cols, channels), BF16)] * 4
        + [pltpu.VMEM((taps, cols), F32), pltpu.SemaphoreType.DMA((5,))],
    )
    sources = [
        pltpu.with_memory_space_constraint(x, pltpu.HBM)
        for x in (values, gate_in, cotangent, gate_out, filters)
    ]
    sent = to_all(pack(*sources))

    transform = vmem_call(
        spectra_kernel,
        jax.ShapeDtypeStruct((shards, wide), BF16),
        2 * shards * wide * (2 * cols + 4 * shards),
        4 * shards * wide,
    )
    back = to_all(transform(sent, early, late))

    half = cols // 2
    terms = jnp.concatenate([back[:, wide // 2 - half : wide // 2], back[:, wide - half :]], axis=1)
    per_filter = terms.astype(F32).reshape(channels // taps, taps, cols).sum(axis=0)
    parts = per_filter.astype(BF16).reshape(replicas, taps // replicas, cols)
    finish = vmem_call(
        functools.partial(finish_kernel, scale),
        [jax.ShapeDtypeStruct((cols, channels), BF16)] * 3
        + [jax.ShapeDtypeStruct((taps // replicas, cols), F32)],
        12 * cols * channels,
        20 * cols * channels,
    )
    *grads, grad_filters = finish(values, gate_in, cotangent, back, gathered_over_batch(parts))
    return tuple(x[None] for x in grads) + (grad_filters,)


def solution(mesh):
    placed = P(None, "seq", "batch")
    return jax.shard_map(
        body,
        mesh=mesh,
        in_specs=(placed, placed, placed, placed, P(None, "seq")),
        out_specs=(placed, placed, placed, P("batch", "seq")),
        check_vma=False,
    )
```
